32 devices in a mesh: groups: 2 (over x), space: 16 (over z, y, core).
Axes of the slice: x: 2, y: 2, z: 4, core: 2. Of those that a mesh axis runs over, the one named last changes fastest.
Arguments:
- grid_in: bfloat16 [96, 1440, 128], P(('groups', 'space')), parts along dimension 0, may hold values from -6 to 6
- upstream: bfloat16 [96, 1440, 128], P(('groups', 'space')), parts along dimension 0, may hold values from -6 to 6
- mix_weight: bfloat16 [2, 128, 128], replicated, may hold values from -0.375 to 0.375
- degree_filter: bfloat16 [512, 128], replicated, may hold values from 0.25 to 2
Outputs:
- grad_in: bfloat16 [96, 1440, 128], P(('groups', 'space')), parts along dimension 0
- grad_weight: float32 [4, 128, 128], P('groups'), parts along dimension 0
- grad_filter: float32 [1024, 128], P('groups'), parts along dimension 0
The draws below stay inside these ranges and needn't reach their ends.
There are 2 independent parts, one for each index of `groups`. The reference program is written for one: setup_inputs(seed, part) draws one part's arguments, and reference() takes and returns one part's arrays. A program takes and returns all parts, laid end to end along the dimension named above; an argument that names none is the same for every part. Nothing has to cross between parts.
All inputs are finite; a program needn't handle non-finite values.
Results may differ from the reference program's by a relative error of at most 0.02.
Values may be sent and summed in bfloat16 or wider, within the bound.
A program may use at most 128 MiB of HBM per device.

```python
import math
import jax
import jax.numpy as jnp
from jax import lax

C = 128
NLON = 1440
MODES = 512
NLAT = 48


def block_levels(stream_key, dims, cuts, smallest, high):
    def one(position, parts):
        heights = jax.random.uniform(jax.random.fold_in(jax.random.fold_in(stream_key, 6), position), (parts,), jnp.float32, smallest / len(cuts), high / len(cuts))
        return jnp.repeat(jnp.exp(heights), dims[position] // parts).reshape((-1,) + (1,) * (len(dims) - position - 1))

    gain = one(*cuts[0])
    for cut in cuts[1:]:
        gain = gain * one(*cut)
    return gain


def bell_draw(rng, shape, scale, limit, pieces=(), kind=jnp.bfloat16):
    factor_of = block_levels(rng, shape, pieces, -0.22, 0.18) if pieces else 1.0
    array = jax.random.normal(rng, shape, jnp.float32) * scale * factor_of
    return jnp.minimum(jnp.maximum(array, -limit), limit).astype(kind)


def setup_inputs(seed: int = 0, part: int = 0) -> dict:
    key_list = jax.random.split(jax.random.key(seed), 5)
    part_splits = jax.random.split(jax.random.fold_in(key_list[4], part), 5)
    return {
        "grid_in": bell_draw(part_splits[0], (NLAT, NLON, C), 1.0, 6.0, ((0, 16),)),
        "upstream": bell_draw(part_splits[1], (NLAT, NLON, C), 1.0, 6.0, ((0, 16),)),
        "mix_weight": bell_draw(key_list[2], (2, C, C), (2 * C) ** -0.5, 0.375),
        "degree_filter": jnp.clip(jax.random.uniform(key_list[3], (MODES, C), jnp.float32, 0.25, 2.0), 0.25, 2.0).astype(jnp.bfloat16),
    }


def latitude_angles(lat_count):
    lat_index = jnp.arange(lat_count, dtype=jnp.float32)
    return math.pi * (lat_index + 0.5) / lat_count

def latitude_weights(lat_count):
    return math.pi / lat_count * jnp.sin(latitude_angles(lat_count))

def legendre_rows(m_values, lat_count, mode_count):
    angles = latitude_angles(lat_count)
    cosine = jnp.cos(angles)[None, :]
    sine_lat = jnp.sin(angles)[None, :]
    orders = m_values.astype(jnp.float32)[:, None]
    log_start = 0.5 * (jnp.log(2.0 * orders + 1.0) - math.log(2.0))
    log_start = log_start + 0.5 * (lax.lgamma(2.0 * orders + 1.0) - 2.0 * lax.lgamma(orders + 1.0) - orders * math.log(4.0))
    log_start = log_start + orders * jnp.log(sine_lat)

    def degree_block(carry, block_index):
        p_now, p_prev, log_scale = carry
        outputs = []
        for inner_step in range(32):
            degree = (block_index * 32 + inner_step).astype(jnp.float32)
            active = degree > orders
            denom = jnp.maximum(degree * degree - orders * orders, 1.0)
            coef_a = jnp.sqrt((4.0 * degree * degree - 1.0) / denom)
            lower = jnp.maximum((degree - 1.0) * (degree - 1.0) - orders * orders, 0.0)
            coef_b = jnp.sqrt(lower * (2.0 * degree + 1.0) / (jnp.maximum(2.0 * degree - 3.0, 1.0) * denom))
            p_next = jnp.where(active, coef_a * cosine * p_now - coef_b * p_prev, p_now)
            p_prev = jnp.where(active, p_now, p_prev)
            p_now = p_next
            outputs.append(jnp.where(degree >= orders, p_now * jnp.exp(log_scale), 0.0))
        magnitude = jnp.maximum(jnp.abs(p_now), jnp.abs(p_prev))
        next_carry = (p_now / magnitude, p_prev / magnitude, log_scale + jnp.log(magnitude))
        return (next_carry, jnp.stack(outputs, 1))
    ones_grid = jnp.ones((m_values.shape[0], lat_count), jnp.float32)
    start_carry = (ones_grid, jnp.zeros_like(ones_grid), log_start * ones_grid)
    block_ids = jnp.arange(mode_count // 32, dtype=jnp.int32)
    final_carry, stacked = lax.scan(degree_block, start_carry, block_ids)
    return jnp.transpose(stacked, (1, 0, 2, 3)).reshape(m_values.shape[0], mode_count, lat_count)

def fourier_tables(m_order, lon_count):
    lon_index = jnp.arange(lon_count, dtype=jnp.int32)
    phases = m_order[:, None] * lon_index[None, :] % lon_count
    angles = 2.0 * math.pi / lon_count * phases.astype(jnp.float32)
    factor = 1.0 / math.sqrt(lon_count)
    analysis = jnp.stack([jnp.cos(angles) * factor, -jnp.sin(angles) * factor], 1)
    analysis = analysis.reshape(2 * m_order.shape[0], lon_count).astype(jnp.bfloat16)
    doubling = jnp.where(m_order == 0, 1.0, 2.0).astype(jnp.bfloat16)
    synthesis = analysis * jnp.repeat(doubling, 2)[:, None]
    return (analysis, synthesis)

def mixing_matrix(mix_weight):
    upper = jnp.concatenate([mix_weight[0], mix_weight[1]], 1)
    lower = jnp.concatenate([-mix_weight[1], mix_weight[0]], 1)
    return jnp.concatenate([upper, lower], 0)

def fold_weight(block_grad):
    half = block_grad.shape[0] // 2
    real_part = block_grad[:half, :half] + block_grad[half:, half:]
    imag_part = block_grad[:half, half:] - block_grad[half:, :half]
    return jnp.stack([real_part, imag_part], 0)

def gelu_slope(field):
    return 0.5 * (1.0 + lax.erf(field * (1.0 / math.sqrt(2.0)))) + field * jnp.exp(-0.5 * field * field) * (1.0 / math.sqrt(2.0 * math.pi))

def product(form, left, right):
    return jnp.einsum(form, left.astype(jnp.float32), right.astype(jnp.float32), precision=lax.Precision.HIGHEST)

def reference(grid_in, upstream, mix_weight, degree_filter):
    lat_count, lon_count, channels = grid_in.shape
    positions = jnp.arange(MODES, dtype=jnp.int32)
    analysis, synthesis = fourier_tables(positions, lon_count)
    wide_weight = mixing_matrix(mix_weight)
    filter_gain = degree_filter.astype(jnp.float32)
    lat_weight = latitude_weights(lat_count)
    block_count = MODES // 32
    block_ids = jnp.arange(block_count, dtype=jnp.int32)
    fourier = product('kn,anc->akc', analysis, grid_in).astype(jnp.bfloat16)
    fourier_blocks = jnp.transpose(fourier.reshape(lat_count, block_count, 32, 2 * channels), (1, 0, 2, 3))

    def forward_pass(block_index, fourier_part):
        m_values = block_index * 32 + jnp.arange(32, dtype=jnp.int32)
        legendre = legendre_rows(m_values, lat_count, MODES)
        synth_table = legendre.astype(jnp.bfloat16)
        anal_table = (legendre * lat_weight).astype(jnp.bfloat16)
        spectrum = product('jla,ajx->jlx', anal_table, fourier_part).astype(jnp.bfloat16)
        scaled = (spectrum.reshape(32, MODES, 2, channels).astype(jnp.float32) * filter_gain[None, :, None, :]).astype(jnp.bfloat16)
        scaled_rows = scaled.reshape(32 * MODES, 2 * channels)
        mixed = jnp.dot(scaled_rows, wide_weight, preferred_element_type=jnp.float32).astype(jnp.bfloat16)
        return (synth_table, anal_table, spectrum, scaled_rows, mixed)

    def forward_block(operands):
        block_index, fourier_part = operands
        synth_table, anal_table, spectrum, scaled_rows, mixed = forward_pass(block_index, fourier_part)
        return product('jla,jlx->ajx', synth_table, mixed.reshape(32, MODES, 2 * channels)).astype(jnp.bfloat16)
    returned = lax.map(forward_block, (block_ids, fourier_blocks))
    returned = jnp.transpose(returned, (1, 0, 2, 3)).reshape(lat_count, 2 * MODES, channels)
    field = product('kn,akc->anc', synthesis, returned)
    slope = (upstream.astype(jnp.float32) * gelu_slope(field)).astype(jnp.bfloat16)
    gfourier = product('kn,anc->akc', synthesis, slope).astype(jnp.bfloat16)
    gradient_blocks = jnp.transpose(gfourier.reshape(lat_count, block_count, 32, 2 * channels), (1, 0, 2, 3))

    def backward_block(operands):
        block_index, fourier_part, gradient_part = operands
        synth_table, anal_table, spectrum, scaled_rows, mixed = forward_pass(block_index, fourier_part)
        gmixed = product('jla,ajx->jlx', synth_table, gradient_part).astype(jnp.bfloat16)
        gmixed_rows = gmixed.reshape(32 * MODES, 2 * channels)
        weight_part = lax.dot_general(scaled_rows, gmixed_rows, (((0,), (0,)), ((), ())), preferred_element_type=jnp.float32)
        gscaled = lax.dot_general(gmixed_rows, wide_weight, (((1,), (1,)), ((), ())), preferred_element_type=jnp.float32)
        gscaled = gscaled.reshape(32, MODES, 2, channels)
        filter_part = lax.optimization_barrier(jnp.sum(gscaled * spectrum.reshape(32, MODES, 2, channels).astype(jnp.float32), axis=(0, 2)))
        gspectrum = (gscaled * filter_gain[None, :, None, :]).astype(jnp.bfloat16).reshape(32, MODES, 2 * channels)
        gfield = product('jla,jlx->ajx', anal_table, gspectrum).astype(jnp.bfloat16)
        return (gfield, weight_part, filter_part)
    gfields, weight_parts, filter_parts = lax.map(backward_block, (block_ids, fourier_blocks, gradient_blocks))
    gfields = jnp.transpose(gfields, (1, 0, 2, 3)).reshape(lat_count, 2 * MODES, channels)
    grad_in = (product('kn,akc->anc', analysis, gfields) + upstream.astype(jnp.float32)).astype(jnp.bfloat16)
    grad_weight = fold_weight(lax.optimization_barrier(jnp.sum(weight_parts, 0))) * (1.0 / MODES)
    grad_filter = lax.optimization_barrier(jnp.sum(filter_parts, 0)) * 0.125
    return (grad_in, grad_weight, grad_filter)
```

```python
import functools
import math

import jax
import jax.numpy as jnp
import numpy as np
from jax import lax
from jax.experimental import pallas as pl
from jax.experimental.pallas import tpu as pltpu
from jax.sharding import PartitionSpec as P

MODES = 512
ROWS = 32
F32 = jnp.float32
BF16 = jnp.bfloat16


def params(**extra):
    return pltpu.CompilerParams(vmem_limit_bytes=56 * 1024 * 1024, **extra)


def latitude_angles(index, lat_count):
    return math.pi * (index.astype(F32) + 0.5) / lat_count


def greet(devices):
    me = lax.axis_index("space")
    barrier = pltpu.get_barrier_semaphore()

    def hello(step, carry):
        peer = (me + step) % devices
        pl.semaphore_signal(
            barrier, inc=1, device_id={"space": peer}, device_id_type=pl.DeviceIdType.MESH
        )
        return carry

    lax.fori_loop(1, devices, hello, 0)


def await_greetings(devices):
    pl.semaphore_wait(pltpu.get_barrier_semaphore(), devices - 1)


def remote(src, dst, send_sem, recv_sem, peer):
    return pltpu.make_async_remote_copy(
        src_ref=src,
        dst_ref=dst,
        send_sem=send_sem,
        recv_sem=recv_sem,
        device_id={"space": peer},
        device_id_type=pl.DeviceIdType.MESH,
    )


class Exchange:
    def __init__(self, source, target, send_sem, recv_sem):
        self.source, self.target = source, target
        self.send_sem, self.recv_sem = send_sem, recv_sem
        self.devices = source.shape[0]
        self.me = lax.axis_index("space")
        self.started = []

    def copy(self, first, last, step):
        peer = (self.me + step) % self.devices
        held = pl.ds(first, last - first)
        return remote(
            self.source.at[peer, held],
            self.target.at[self.me, held],
            self.send_sem.at[first, step],
            self.recv_sem.at[first, step],
            peer,
        )

    def send(self, first, last):
        half = self.devices // 2

        def one(index, carry):
            sign = 1 - 2 * (index % 2)
            step = (half + sign * ((index + 1) // 2) + self.devices) % self.devices
            self.copy(first, last, step).start()
            return carry

        lax.fori_loop(0, self.devices - 1, one, 0)
        self.started.append((first, last))
        held = pl.ds(first, last - first)
        self.target[self.me, held] = self.source[self.me, held]

    def arrive(self, first, last):
        def one(step, carry):
            self.copy(first, last, step).wait_recv()
            return carry

        lax.fori_loop(1, self.devices, one, 0)

    def drain(self):
        for first, last in self.started:

            def one(step, carry, first=first, last=last):
                self.copy(first, last, step).wait_send()
                return carry

            lax.fori_loop(1, self.devices, one, 0)


def radices_of(devices):
    radices = []
    while devices > 1:
        radix = 8 if devices % 8 == 0 and radices else 2
        radix = radix if devices % radix == 0 else devices
        radices.append(radix)
        devices //= radix
    return radices


class Reduction:
    def __init__(self, red, stage, inbox, total, send_sem, recv_sem):
        self.red, self.stage, self.inbox, self.total = red, stage, inbox, total
        self.send_sem, self.recv_sem = send_sem, recv_sem
        count = red.shape[0]
        self.me = lax.axis_index("space")
        self.levels = []
        base = self.me * 0
        stride = 1
        offset = 0
        for radix in radices_of(count):
            count //= radix
            digit = self.me // stride % radix
            self.levels.append((radix, stride, digit, count, base, offset))
            base = base + digit * count
            offset += (radix - 1) * count
            stride *= radix
        self.base = base

    def scatter_copies(self, level):
        radix, stride, digit, count, base, offset = self.levels[level]
        span = pl.ds(base, radix * count)
        self.stage[span] = self.red[span].astype(BF16)
        copies = []
        for k in range(1, radix):
            other = (digit + k) % radix
            copies.append(
                remote(
                    self.stage.at[pl.ds(base + other * count, count)],
                    self.inbox.at[pl.ds(offset + (k - 1) * count, count)],
                    self.send_sem.at[0, level, k],
                    self.recv_sem.at[0, level, k],
                    self.me + (other - digit) * stride,
                )
            )
        return copies

    def scatter_end(self, level, copies):
        radix, _, digit, count, base, offset = self.levels[level]
        for copy in copies:
            copy.wait()
        keep = pl.ds(base + digit * count, count)
        value = self.red[keep]
        for k in range(1, radix):
            low = offset + (k - 1) * count
            value = value + self.inbox[low : low + count].astype(F32)
        if level == len(self.levels) - 1:
            self.total[keep] = value.astype(BF16)
        else:
            self.red[keep] = value

    def gather_copies(self, level):
        radix, stride, digit, count, base, _ = self.levels[level]
        block = self.total.at[pl.ds(base + digit * count, count)]
        copies = []
        for k in range(1, radix):
            other = (digit + k) % radix
            copies.append(
                remote(
                    block,
                    block,
                    self.send_sem.at[1, level, k],
                    self.recv_sem.at[1, level, k],
                    self.me + (other - digit) * stride,
                )
            )
        return copies

    def gather_end(self, level, copies):
        for copy in copies:
            copy.wait()

    def steps(self):
        count = len(self.levels)
        steps = [(self.scatter_copies, self.scatter_end, t) for t in range(count)]
        return steps + [(self.gather_copies, self.gather_end, t) for t in reversed(range(count))]


def sections_of(devices):
    return max(1, min(4, MODES // devices // 8))


def row_phase(rows, devices, lon_count):
    span = 2 * MODES // devices // sections_of(devices)
    section = rows // (span * devices)
    device = rows // span % devices
    part = rows // (span // 2) % 2
    slot = section * (span // 2) + rows % (span // 2)
    return slot * devices + device, part * (lon_count // 4)


def cosine_of(phase, lon_count):
    turn = phase - jnp.floor(phase * (1.0 / lon_count)) * lon_count
    x = (lon_count / 4 - jnp.abs(turn - lon_count / 2)) * (2.0 * math.pi / lon_count)
    y = x * x
    tail = 1.0 / 362880.0 - y * (1.0 / 39916800.0)
    tail = 1.0 / 120.0 + y * (-1.0 / 5040.0 + y * tail)
    return -x * (1.0 + y * (-1.0 / 6.0 + y * tail))


def angle_indices(devices, lon_count):
    order, offset = row_phase(np.arange(2 * MODES), devices, lon_count)

    def column(values):
        return np.broadcast_to(values.astype(np.float32)[:, None], (len(values), 128))

    def lanes(values):
        return np.broadcast_to(values.astype(np.float32)[None, :], (8, len(values)))

    columns = np.stack([column(v) for v in (order[::ROWS], offset[::ROWS], order[:ROWS], offset[:ROWS])])
    return jnp.asarray(columns), jnp.asarray(np.stack([lanes(order), lanes(offset)]))


def angles_by_row(columns, lon_count, big, small):
    rows = big.shape[1]
    lon = lax.broadcasted_iota(jnp.int32, (rows, lon_count), 1).astype(F32)
    phase = columns[0][:, 0:1] * lon + columns[1][:, 0:1]
    big[0] = cosine_of(phase, lon_count)
    big[1] = cosine_of(phase + 0.75 * lon_count, lon_count)
    lon = lax.broadcasted_iota(jnp.int32, (ROWS, lon_count), 1).astype(F32)
    phase = columns[2][:, 0:1] * lon + columns[3][:, 0:1]
    factor = 1.0 / math.sqrt(lon_count)
    small[0] = cosine_of(phase, lon_count) * factor
    small[1] = cosine_of(phase + 0.75 * lon_count, lon_count) * factor


def angles_by_lane(lanes, lon_count, big, small):
    rows, total = big.shape[1:]
    order, offset = lanes[0, 0:1, :], lanes[1, 0:1, :]
    lon = lax.broadcasted_iota(jnp.int32, (rows, total), 0).astype(F32) * float(ROWS)
    phase = lon * order
    big[0] = cosine_of(phase, lon_count)
    big[1] = cosine_of(phase + 0.75 * lon_count, lon_count)
    lon = lax.broadcasted_iota(jnp.int32, (ROWS, total), 0).astype(F32)
    phase = lon * order + offset
    factor = 1.0 / math.sqrt(lon_count)
    small[0] = cosine_of(phase, lon_count) * factor
    small[1] = cosine_of(phase + 0.75 * lon_count, lon_count) * factor


def fill(dst, big, small, first, last):
    def step(h, carry):
        value = big[0, pl.ds(h, 1), :] * small[0] - big[1, pl.ds(h, 1), :] * small[1]
        dst[pl.ds(pl.multiple_of(h * ROWS, ROWS), ROWS), :] = value.astype(BF16)
        return carry

    lax.fori_loop(first, last, step, 0)


def alpha_column(section, rows, span):
    row = lax.broadcasted_iota(jnp.int32, (rows, 128), 0)
    zero = jnp.logical_or(row == 0, row == span // 2)
    alpha = jnp.where(zero, 1.0, 2.0) if section == 0 else jnp.full((rows, 128), 2.0, F32)
    return alpha[:, 0:1]


def section_product(table, wide, out, section, lanes, scaled):
    devices, _, span, width = out.shape
    count = devices * span
    chunk = 256
    each = chunk // span
    for q in range(count // chunk):
        first = section * count + q * chunk
        value = jnp.dot(
            table[first : first + chunk, :], wide[:, lanes], preferred_element_type=F32
        )
        if scaled:
            value = value * (alpha_column(0, chunk, span) if first == 0 else 2.0)
        out[q * each : (q + 1) * each, section] = value.astype(BF16).reshape(each, span, width)


def legendre_tables(
    slot_ref, start_ref, lat_ref, synth, anal, tsynth, tanal, hold
):
    groups, width = slot_ref.shape
    orders = slot_ref[...] + lax.axis_index("space").astype(F32)
    order_sq = orders * orders
    cosine = lat_ref[0:1, :]
    wrow = lat_ref[1:2, :]
    wcol = jnp.broadcast_to(wrow, (128, width)).T[:, 0:1]
    block = 32

    def degree_block(index, carry):
        p_now, p_prev, e_prev, log_scale = carry
        scale = jnp.exp(log_scale)
        base = index * block
        for inner in range(block):
            degree_int = base + inner
            degree = degree_int.astype(F32)
            active = degree > orders
            square = degree * degree
            ratio = jnp.maximum(square - order_sq, 1.0) / jnp.maximum(4.0 * square - 1.0, 1.0)
            coef = lax.rsqrt(ratio)
            p_next = jnp.where(active, coef * (cosine * p_now - e_prev * p_prev), p_now)
            p_prev = jnp.where(active, p_now, p_prev)
            e_prev = jnp.where(active, ratio * coef, 0.0)
            p_now = p_next
            value = jnp.where(degree >= orders, p_now * scale, 0.0)
            rows = pl.ds(pl.multiple_of(degree_int * groups, groups), groups)
            for part in range(width // 128):
                hold[part, rows, :] = value[:, part * 128 : (part + 1) * 128]
        magnitude = jnp.maximum(jnp.abs(p_now), jnp.abs(p_prev))
        return (p_now / magnitude, p_prev / magnitude, e_prev, log_scale + jnp.log(magnitude))

    ones = jnp.ones((groups, width), F32)
    zeros = jnp.zeros((groups, width), F32)
    lax.fori_loop(0, MODES // block, degree_block, (ones, zeros, zeros, start_ref[...]))

    def spread(g, carry):
        pieces = [
            hold[part, pl.ds(g, MODES, stride=groups), :]
            for part in range(width // 128)
        ]
        value = pieces[0] if len(pieces) == 1 else jnp.concatenate(pieces, 1)
        synth[g] = value.astype(BF16)
        anal[g] = (value * wrow).astype(BF16)
        turned = value.T
        tsynth[g] = turned.astype(BF16)
        tanal[g] = (turned * wcol).astype(BF16)
        return carry

    lax.fori_loop(0, synth.shape[0], spread, 0)


def unpack(sources, parts, scratch, q):
    for src, (low, high) in zip(sources, parts):
        devices, _, span, _ = src.shape
        for a in range(low, high):
            part = src[:, q, :, (a - low) * 128 : (a - low + 1) * 128].astype(F32)
            scratch[a, q * devices * span : (q + 1) * devices * span] = part.reshape(
                devices * span, 128
            )


def pack(scratch, targets, parts, q):
    for dst, (low, high) in zip(targets, parts):
        devices, _, span, _ = dst.shape
        for a in range(low, high):
            part = scratch[a, q * devices * span : (q + 1) * devices * span]
            dst[:, q, :, (a - low) * 128 : (a - low + 1) * 128] = part.reshape(
                devices, span, 128
            ).astype(BF16)


def strided_rows(s, r, devices, span):
    half = span // 2
    start = s // half * (devices * span) + r * half + s % half
    return pl.ds(start, devices, stride=span)


def gather_group(scratch, g, devices, span, per_group, height):
    lat_local = scratch.shape[0]
    rows = []
    for j in range(per_group):
        s = g * per_group + j
        halves = []
        for r in range(2):
            pick = strided_rows(s, r, devices, span)
            parts = [scratch[a, pick, :] for a in range(lat_local)]
            if height > devices * lat_local:
                parts.append(jnp.zeros((height - devices * lat_local, 128), F32))
            halves.append(jnp.concatenate(parts, 0))
        zero = jnp.zeros((height, 256), F32)
        cells = [zero] * per_group
        cells[j] = jnp.concatenate(halves, 1)
        rows.append(cells[0] if per_group == 1 else jnp.concatenate(cells, 1))
    return (rows[0] if per_group == 1 else jnp.concatenate(rows, 0)).astype(BF16)


def scatter_group(value, scratch, g, devices, span, per_group, height):
    lat_local = scratch.shape[0]
    for j in range(per_group):
        s = g * per_group + j
        for r in range(2):
            for a in range(lat_local):
                top = j * height + a * devices
                left = j * 256 + r * 128
                scratch[a, strided_rows(s, r, devices, span), :] = value[
                    top : top + devices, left : left + 128
                ]


def over_groups(groups, sections, section, body):
    pieces = 4
    each = groups // pieces
    share = pieces // sections
    for q in range(section * share, (section + 1) * share):
        first = q * (MODES // pieces)
        lax.fori_loop(q * each, (q + 1) * each, functools.partial(body, first), 0)


def widen(filter_ref, first, copies):
    gain = filter_ref[first:, :].astype(F32)
    return jnp.concatenate([gain] * copies, 1)


def forward_body(per_group, shapes, anal, tsynth, filt, weight, scratch, back):
    devices, _, span, _ = shapes
    height = anal.shape[2] // per_group

    def body(first, g, carry):
        operand = gather_group(scratch, g, devices, span, per_group, height)
        spectrum = jnp.dot(anal[g, first:, :], operand, preferred_element_type=F32).astype(BF16)
        scaled = (spectrum.astype(F32) * widen(filt, first, 2 * per_group)).astype(BF16)
        mixed = [
            jnp.dot(
                scaled[:, j * 256 : (j + 1) * 256], weight[...], preferred_element_type=F32
            ).astype(BF16)
            for j in range(per_group)
        ]
        mixed = mixed[0] if per_group == 1 else jnp.concatenate(mixed, 1)
        value = jnp.dot(tsynth[g, :, first:], mixed, preferred_element_type=F32)
        scatter_group(value, back, g, devices, span, per_group, height)
        return carry

    return body


def backward_body(
    per_group, shapes, anal, synth, tanal, filt, weight, scratch, gscratch, wgrad, fgrad
):
    devices, _, span, _ = shapes
    height = anal.shape[2] // per_group

    def body(first, g, carry):
        operand = gather_group(scratch, g, devices, span, per_group, height)
        goperand = gather_group(gscratch, g, devices, span, per_group, height)
        gain = widen(filt, first, 2)
        outs = []
        spectrum = jnp.dot(anal[g, first:, :], operand, preferred_element_type=F32).astype(BF16)
        gmixed = jnp.dot(synth[g, first:, :], goperand, preferred_element_type=F32).astype(BF16)
        for j in range(per_group):
            lanes = slice(j * 256, (j + 1) * 256)
            spec = spectrum[:, lanes].astype(F32)
            scaled = (spec * gain).astype(BF16)
            gmix = gmixed[:, lanes]
            wgrad[...] += lax.dot_general(
                scaled, gmix, (((0,), (0,)), ((), ())), preferred_element_type=F32
            )
            gscaled = lax.dot_general(
                gmix, weight[...], (((1,), (1,)), ((), ())), preferred_element_type=F32
            )
            term = gscaled * spec
            fgrad[first:, :] += term[:, :128] + term[:, 128:]
            outs.append((gscaled * gain).astype(BF16))
        gspectrum = outs[0] if per_group == 1 else jnp.concatenate(outs, 1)
        value = jnp.dot(tanal[g, :, first:], gspectrum, preferred_element_type=F32)
        scatter_group(value, scratch, g, devices, span, per_group, height)
        return carry

    return body


def fold_gradients(wgrad, fgrad, red):
    half = wgrad.shape[0] // 2
    pieces = [
        (wgrad[:half, :half] + wgrad[half:, half:]) * (1.0 / MODES),
        (wgrad[:half, half:] - wgrad[half:, :half]) * (1.0 / MODES),
        fgrad[...] * 0.125,
    ]
    spare = red.shape[0] * red.shape[1] - 2 * half - MODES
    if spare:
        pieces.append(jnp.zeros((spare, 128), F32))
    red[...] = jnp.concatenate(pieces, 0).reshape(red.shape)


def gelu_slope(field):
    return 0.5 * (1.0 + lax.erf(field * (1.0 / math.sqrt(2.0)))) + field * jnp.exp(
        -0.5 * field * field
    ) * (1.0 / math.sqrt(2.0 * math.pi))


LON_CHUNK = 288


def merged(src, first, last, scaled):
    devices, _, span, width = src.shape
    pieces = []
    for q in range(first, last):
        value = src[:, q].astype(F32).reshape(devices * span, width)
        if scaled:
            value = value * alpha_column(q, devices * span, span)
        pieces.append(value.astype(BF16))
    return pieces[0] if len(pieces) == 1 else jnp.concatenate(pieces, 0)


def add_sections(ttable, operand, first, field, lanes, last):
    count = operand.shape[0]
    lon_count = field.shape[0]

    def grid_rows(q, carry):
        rows = pl.ds(pl.multiple_of(q * LON_CHUNK, LON_CHUNK), LON_CHUNK)
        value = jnp.dot(
            ttable[rows, first : first + count], operand, preferred_element_type=F32
        )
        if first:
            value = value + field[rows, lanes]
        if last is None:
            field[rows, lanes] = value
        else:
            last(q, rows, value)
        return carry

    lax.fori_loop(0, lon_count // LON_CHUNK, grid_rows, 0)


def lat_parts(lat_local):
    tail = max(1, lat_local // 3)
    if lat_local <= tail:
        return [(0, lat_local)]
    return [(0, lat_local - tail), (lat_local - tail, lat_local)]


def lane_slice(part):
    return slice(part[0] * 128, part[1] * 128)


def block_kernel(
    per_group,
    columns_hbm, lanes_hbm, grid_hbm, upstream_hbm, slots_hbm, start_hbm, lats_hbm, filt_hbm, mix_hbm,
    grad_hbm, sums_hbm,
    columns, lanes, grid, upstream, slots, start, lats, filt, mix_weight, grad,
    weight, total, table, ttable, big, small, tbig, tsmall,
    synth, anal, tsynth, tanal, hold,
    scratch, back, field, slope, wgrad, fgrad, red, stage, inbox,
    rsend, rrecv, lsem, osem,
    *buffers,
):
    lat_local = grid_hbm.shape[0]
    parts = lat_parts(lat_local)
    whole = [(0, lat_local)]
    split = len(parts)
    exchanges = [Exchange(*buffers[k : k + 4]) for k in range(0, len(buffers), 4)]
    first, fourth = exchanges[:2]
    second, third = exchanges[2 : 2 + split], exchanges[2 + split :]
    shapes = first.source.shape
    devices, sections, span, _ = shapes
    halves = [(0, sections // 2), (sections // 2, sections)] if sections > 1 else [(0, 1)]
    lat_local, lon_count, channels = grid_hbm.shape
    groups = synth.shape[0]
    me = lax.axis_index("space")
    greet(devices)

    loads = {}

    def load(name, src, dst):
        copy = pltpu.make_async_copy(src, dst, lsem.at[len(loads)])
        copy.start()
        loads[name] = copy

    load("columns", columns_hbm, columns)
    for a in range(lat_local):
        load(("grid", a), grid_hbm.at[a], grid.at[:, a * 128 : (a + 1) * 128])
    load("slots", slots_hbm, slots)
    load("start", start_hbm.at[me], start)
    load("lats", lats_hbm, lats)
    load("filt", filt_hbm, filt)
    load("mix", mix_hbm, mix_weight)
    load("lanes", lanes_hbm, lanes)
    for a in range(lat_local):
        load(("up", a), upstream_hbm.at[a], upstream.at[:, a * 128 : (a + 1) * 128])

    everything = slice(0, lat_local * 128)
    loads["columns"].wait()
    angles_by_row(columns, lon_count, big, small)
    share = big.shape[1] // sections
    for q in range(sections):
        fill(table, big, small, q * share, (q + 1) * share)
        if q == 0:
            for a in range(lat_local):
                loads["grid", a].wait()
        section_product(table, grid, first.source, q, everything, False)
        if q == 0:
            await_greetings(devices)
        first.send(q, q + 1)
    for name in ("slots", "start", "lats", "filt", "mix", "lanes"):
        loads[name].wait()
    weight[:channels, :channels] = mix_weight[0]
    weight[:channels, channels:] = mix_weight[1]
    weight[channels:, :channels] = -mix_weight[1]
    weight[channels:, channels:] = mix_weight[0]
    legendre_tables(slots, start, lats, synth, anal, tsynth, tanal, hold)

    forward = forward_body(per_group, shapes, anal, tsynth, filt, weight, scratch, back)
    for low, high in halves:
        for q in range(low, high):
            first.arrive(q, q + 1)
            unpack([first.target], whole, scratch, q)
            over_groups(groups, sections, q, forward)
            pack(back, [exchange.source for exchange in second], parts, q)
        second[0].send(low, high)
    for exchange in second[1:]:
        exchange.send(0, sections)
    angles_by_lane(lanes, lon_count, tbig, tsmall)
    fill(ttable, tbig, tsmall, 0, tbig.shape[1])
    for a in range(lat_local):
        loads["up", a].wait()

    def gate(where, q, rows, value):
        up = upstream[rows, where].astype(F32)
        slope[rows, where] = (up * gelu_slope(value)).astype(BF16)

    for p, part in enumerate(parts):
        where = lane_slice(part)
        close = functools.partial(gate, where)
        for low, high in halves if p == 0 else [(0, sections)]:
            second[p].arrive(low, high)
            operand = merged(second[p].target, low, high, True)
            last = close if high == sections else None
            add_sections(ttable, operand, low * devices * span, field, where, last)
        for low, high in halves:
            for q in range(low, high):
                section_product(table, slope, third[p].source, q, where, True)
            if p == 0 and low == 0 or split == 1:
                third[p].send(low, high)
            if p == split - 1 and p > 0:
                for exchange in third if low else third[1:]:
                    exchange.send(low, high)

    wgrad[...] = jnp.zeros_like(wgrad)
    fgrad[...] = jnp.zeros_like(fgrad)
    backward = backward_body(
        per_group, shapes, anal, synth, tanal, filt, weight, scratch, back, wgrad, fgrad
    )
    for low, high in halves:
        for exchange in third:
            exchange.arrive(low, high)
        for q in range(low, high):
            unpack([exchange.target for exchange in third], parts, back, q)
            over_groups(groups, sections, q, backward)
            pack(scratch, [fourth.source], whole, q)
            if low == 0 and sections > 1:
                fourth.send(q, q + 1)
    fold_gradients(wgrad, fgrad, red)
    reduction = Reduction(red, stage, inbox, total, rsend, rrecv)

    def out_copy(q, a, rows):
        return pltpu.make_async_copy(
            grad.at[rows, a * 128 : (a + 1) * 128], grad_hbm.at[a, rows, :], osem.at[q, a]
        )

    def finish(q, rows, value):
        grad[rows, :] = (value + upstream[rows, :].astype(F32)).astype(BF16)
        for a in range(lat_local):
            out_copy(q, a, rows).start()

    def tail(low, high):
        fourth.arrive(low, high)
        operand = merged(fourth.target, low, high, False)
        last = finish if high == sections else None
        add_sections(ttable, operand, low * devices * span, field, everything, last)

    steps = reduction.steps()
    middle = len(steps) // 2
    held = list(range(*halves[-1]))
    sends = {q: min(middle - 1 + k, middle) for k, q in enumerate(held)}
    places = {q: min(middle - 1 + q, len(steps) - 1) for q in range(sections - 1)}
    for index, (begin, end, level) in enumerate(steps):
        copies = begin(level)
        for copy in copies:
            copy.start()
        for q in held:
            if sends[q] == index:
                fourth.send(q, q + 1)
        for q, place in places.items():
            if place == index:
                tail(q, q + 1)
        end(level, copies)
    tail(sections - 1, sections)
    red[...] = total[...].astype(F32)
    sums_copy = pltpu.make_async_copy(red, sums_hbm, lsem.at[len(loads)])
    sums_copy.start()
    for exchange in exchanges:
        exchange.drain()
    for q in range(lon_count // LON_CHUNK):
        rows = pl.ds(q * LON_CHUNK, LON_CHUNK)
        for a in range(lat_local):
            out_copy(q, a, rows).wait()
    sums_copy.wait()


def publish_kernel(grad_in, sums_in, grad, weight, filt, grad_v, sums_v, isem, osem):
    lat_local = grad_in.shape[0]
    pulls = [
        pltpu.make_async_copy(grad_in.at[a], grad_v.at[a], isem.at[a]) for a in range(lat_local)
    ]
    pulls.append(pltpu.make_async_copy(sums_in, sums_v, isem.at[lat_local]))
    for copy in pulls:
        copy.start()
    pushes = []
    for a in range(lat_local):
        pulls[a].wait()
        pushes.append(pltpu.make_async_copy(grad_v.at[a], grad.at[a], osem.at[a]))
        pushes[-1].start()
    pulls[-1].wait()
    rows = weight.shape[1]
    for r in range(weight.shape[0]):
        pushes.append(
            pltpu.make_async_copy(
                sums_v.at[pl.ds(r * rows, rows)], weight.at[r], osem.at[lat_local + r]
            )
        )
    pushes.append(
        pltpu.make_async_copy(
            sums_v.at[pl.ds(2 * rows, filt.shape[0])], filt, osem.at[lat_local + weight.shape[0]]
        )
    )
    for copy in pushes[lat_local:]:
        copy.start()
    for copy in pushes:
        copy.wait()


def order_logs(devices, group_orders, sines):
    scale = []
    for m in range(MODES):
        value = 0.5 * (math.log(2.0 * m + 1.0) - math.log(2.0))
        value += 0.5 * (math.lgamma(2.0 * m + 1.0) - 2.0 * math.lgamma(m + 1.0) - m * math.log(4.0))
        scale.append(value)
    orders = group_orders[None] + np.arange(devices)[:, None, None]
    return (np.array(scale)[orders] + orders * np.log(sines)[None, None, :]).astype(np.float32)


def body(grid_in, upstream, mix_weight, degree_filter):
    devices = lax.axis_size("space")
    me = lax.axis_index("space")
    lat_local, lon_count, channels = grid_in.shape
    lat_count = lat_local * devices
    slots = MODES // devices
    sections = sections_of(devices)
    span = 2 * slots // sections
    height = 64 if lat_count <= 64 else -(-lat_count // 128) * 128
    per_group = 128 // height if height < 128 else 1
    width = height * per_group
    groups = slots // per_group
    dims = (devices, sections, span)

    lane = np.arange(width)
    within = lane % height
    valid = within < lat_count
    latitude = np.where(valid, within % devices * lat_local + within // devices, 0)
    padded = -(-groups // 8) * 8
    group = np.minimum(np.arange(padded), groups - 1)[:, None]
    group_orders = (group * per_group + lane[None, :] // height) * devices
    slot_orders = jnp.asarray(group_orders.astype(np.float32))
    angles = math.pi * (latitude + 0.5) / lat_count
    start = jnp.asarray(order_logs(devices, group_orders, np.sin(angles)))
    weights = math.pi / lat_count * np.sin(angles) * valid
    lats = np.stack([np.cos(angles)] + [weights] * 7).astype(np.float32)
    columns, lanes = angle_indices(devices, lon_count)
    operands = (
        columns, lanes, grid_in, upstream, slot_orders, start, jnp.asarray(lats), degree_filter, mix_weight,
    )

    share = -(-(2 * channels + MODES) // (16 * devices)) * 16
    blocks = (devices, share, channels)
    vmem = pltpu.VMEM
    slab = vmem((lat_local, 2 * MODES, 128), F32)
    total_rows = 2 * MODES
    wide = lat_local * channels
    semaphores = pltpu.SemaphoreType.DMA((sections, devices))
    buffers = []
    for low, high in [(0, lat_local)] * 2 + lat_parts(lat_local) * 2:
        block = vmem((*dims, (high - low) * channels), BF16)
        buffers += [block, block, semaphores, semaphores]
    levels = radices_of(devices)
    hops = pltpu.SemaphoreType.DMA((2, len(levels), max(levels)))
    anywhere = pl.BlockSpec(memory_space=pl.ANY)
    grad, sums = pl.pallas_call(
        functools.partial(block_kernel, per_group),
        out_shape=(
            jax.ShapeDtypeStruct(grid_in.shape, BF16),
            jax.ShapeDtypeStruct(blocks, F32),
        ),
        in_specs=[anywhere] * len(operands),
        out_specs=(anywhere, anywhere),
        scratch_shapes=[
            vmem(columns.shape, F32),
            vmem(lanes.shape, F32),
            vmem((lon_count, wide), BF16),
            vmem((lon_count, wide), BF16),
            vmem(slot_orders.shape, F32),
            vmem(start.shape[1:], F32),
            vmem(lats.shape, F32),
            vmem(degree_filter.shape, BF16),
            vmem(mix_weight.shape, BF16),
            vmem((lon_count, wide), BF16),
            vmem((2 * channels, 2 * channels), BF16),
            vmem(blocks, BF16),
            vmem((total_rows, lon_count), BF16),
            vmem((lon_count, total_rows), BF16),
            vmem((2, total_rows // ROWS, lon_count), F32),
            vmem((2, ROWS, lon_count), F32),
            vmem((2, lon_count // ROWS, total_rows), F32),
            vmem((2, ROWS, total_rows), F32),
            vmem((groups, MODES, width), BF16),
            vmem((groups, MODES, width), BF16),
            vmem((groups, width, MODES), BF16),
            vmem((groups, width, MODES), BF16),
            vmem((width // 128, MODES * padded, 128), F32),
            slab,
            slab,
            vmem((lon_count, wide), F32),
            vmem((lon_count, wide), BF16),
            vmem((2 * channels, 2 * channels), F32),
            vmem((MODES, channels), F32),
            vmem(blocks, F32),
            vmem(blocks, BF16),
            vmem(blocks, BF16),
            hops,
            hops,
            pltpu.SemaphoreType.DMA((16 + 2 * lat_local,)),
            pltpu.SemaphoreType.DMA((lon_count // LON_CHUNK, lat_local)),
            *buffers,
        ],
        compiler_params=params(collective_id=0, has_side_effects=True),
        name="block",
    )(*operands)
    flat = sums.reshape(devices * share, channels)
    return pl.pallas_call(
        publish_kernel,
        out_shape=(
            jax.ShapeDtypeStruct(grid_in.shape, BF16),
            jax.ShapeDtypeStruct(mix_weight.shape, F32),
            jax.ShapeDtypeStruct(degree_filter.shape, F32),
        ),
        in_specs=[anywhere, anywhere],
        out_specs=(anywhere,) * 3,
        scratch_shapes=[
            vmem(grid_in.shape, BF16),
            vmem(flat.shape, F32),
            pltpu.SemaphoreType.DMA((lat_local + 1,)),
            pltpu.SemaphoreType.DMA((lat_local + 3,)),
        ],
        name="publish",
    )(grad, flat)


def solution(mesh):
    return jax.shard_map(
        body,
        mesh=mesh,
        in_specs=(P(("groups", "space"), None, None), P(("groups", "space"), None, None), P(), P()),
        out_specs=(P(("groups", "space"), None, None), P("groups", None, None), P("groups", None)),
        check_vma=False,
    )
```

```python
import functools
import math

import jax
import jax.numpy as jnp
import numpy as np
from jax import lax
from jax.experimental import pallas as pl
from jax.experimental.pallas import tpu as pltpu
from jax.sharding import PartitionSpec as P

MODES = 512
ROWS = 32
F32 = jnp.float32
BF16 = jnp.bfloat16


def params(**extra):
    return pltpu.CompilerParams(vmem_limit_bytes=56 * 1024 * 1024, **extra)


def latitude_angles(index, lat_count):
    return math.pi * (index.astype(F32) + 0.5) / lat_count


def greet(devices):
    me = lax.axis_index("space")
    barrier = pltpu.get_barrier_semaphore()

    def hello(step, carry):
        peer = (me + step) % devices
        pl.semaphore_signal(
            barrier, inc=1, device_id={"space": peer}, device_id_type=pl.DeviceIdType.MESH
        )
        return carry

    lax.fori_loop(1, devices, hello, 0)


def await_greetings(devices):
    pl.semaphore_wait(pltpu.get_barrier_semaphore(), devices - 1)


def remote(src, dst, send_sem, recv_sem, peer):
    return pltpu.make_async_remote_copy(
        src_ref=src,
        dst_ref=dst,
        send_sem=send_sem,
        recv_sem=recv_sem,
        device_id={"space": peer},
        device_id_type=pl.DeviceIdType.MESH,
    )


class Exchange:
    def __init__(self, source, target, send_sem, recv_sem):
        self.source, self.target = source, target
        self.send_sem, self.recv_sem = send_sem, recv_sem
        self.devices = source.shape[0]
        self.me = lax.axis_index("space")
        self.started = []

    def copy(self, first, last, step):
        peer = (self.me + step) % self.devices
        held = pl.ds(first, last - first)
        return remote(
            self.source.at[peer, held],
            self.target.at[self.me, held],
            self.send_sem.at[first, step],
            self.recv_sem.at[first, step],
            peer,
        )

    def send(self, first, last):
        half = self.devices // 2

        def one(index, carry):
            sign = 1 - 2 * (index % 2)
            step = (half + sign * ((index + 1) // 2) + self.devices) % self.devices
            self.copy(first, last, step).start()
            return carry

        lax.fori_loop(0, self.devices - 1, one, 0)
        self.started.append((first, last))
        held = pl.ds(first, last - first)
        self.target[self.me, held] = self.source[self.me, held]

    def arrive(self, first, last):
        def one(step, carry):
            self.copy(first, last, step).wait_recv()
            return carry

        lax.fori_loop(1, self.devices, one, 0)

    def drain(self):
        for first, last in self.started:

            def one(step, carry, first=first, last=last):
                self.copy(first, last, step).wait_send()
                return carry

            lax.fori_loop(1, self.devices, one, 0)


def radices_of(devices):
    radices = []
    while devices > 1:
        radix = 8 if devices % 8 == 0 and radices else 2
        radix = radix if devices % radix == 0 else devices
        radices.append(radix)
        devices //= radix
    return radices


class Reduction:
    def __init__(self, red, stage, inbox, total, send_sem, recv_sem):
        self.red, self.stage, self.inbox, self.total = red, stage, inbox, total
        self.send_sem, self.recv_sem = send_sem, recv_sem
        count = red.shape[0]
        self.me = lax.axis_index("space")
        self.levels = []
        base = self.me * 0
        stride = 1
        offset = 0
        for radix in radices_of(count):
            count //= radix
            digit = self.me // stride % radix
            self.levels.append((radix, stride, digit, count, base, offset))
            base = base + digit * count
            offset += (radix - 1) * count
            stride *= radix
        self.base = base

    def scatter_copies(self, level):
        radix, stride, digit, count, base, offset = self.levels[level]
        span = pl.ds(base, radix * count)
        self.stage[span] = self.red[span].astype(BF16)
        copies = []
        for k in range(1, radix):
            other = (digit + k) % radix
            copies.append(
                remote(
                    self.stage.at[pl.ds(base + other * count, count)],
                    self.inbox.at[pl.ds(offset + (k - 1) * count, count)],
                    self.send_sem.at[0, level, k],
                    self.recv_sem.at[0, level, k],
                    self.me + (other - digit) * stride,
                )
            )
        return copies

    def scatter_end(self, level, copies):
        radix, _, digit, count, base, offset = self.levels[level]
        for copy in copies:
            copy.wait()
        keep = pl.ds(base + digit * count, count)
        value = self.red[keep]
        for k in range(1, radix):
            low = offset + (k - 1) * count
            value = value + self.inbox[low : low + count].astype(F32)
        if level == len(self.levels) - 1:
            self.total[keep] = value.astype(BF16)
        else:
            self.red[keep] = value

    def gather_copies(self, level):
        radix, stride, digit, count, base, _ = self.levels[level]
        block = self.total.at[pl.ds(base + digit * count, count)]
        copies = []
        for k in range(1, radix):
            other = (digit + k) % radix
            copies.append(
                remote(
                    block,
                    block,
                    self.send_sem.at[1, level, k],
                    self.recv_sem.at[1, level, k],
                    self.me + (other - digit) * stride,
                )
            )
        return copies

    def gather_end(self, level, copies):
        for copy in copies:
            copy.wait()

    def steps(self):
        count = len(self.levels)
        steps = [(self.scatter_copies, self.scatter_end, t) for t in range(count)]
        return steps + [(self.gather_copies, self.gather_end, t) for t in reversed(range(count))]


def sections_of(devices):
    return max(1, min(4, MODES // devices // 8))


def row_phase(rows, devices, lon_count):
    span = 2 * MODES // devices // sections_of(devices)
    section = rows // (span * devices)
    device = rows // span % devices
    part = rows // (span // 2) % 2
    slot = section * (span // 2) + rows % (span // 2)
    return slot * devices + device, part * (lon_count // 4)


def cosine_of(phase, lon_count):
    turn = phase - jnp.floor(phase * (1.0 / lon_count)) * lon_count
    x = (lon_count / 4 - jnp.abs(turn - lon_count / 2)) * (2.0 * math.pi / lon_count)
    y = x * x
    tail = 1.0 / 362880.0 - y * (1.0 / 39916800.0)
    tail = 1.0 / 120.0 + y * (-1.0 / 5040.0 + y * tail)
    return -x * (1.0 + y * (-1.0 / 6.0 + y * tail))


def angle_indices(devices, lon_count):
    order, offset = row_phase(np.arange(2 * MODES), devices, lon_count)

    def column(values):
        return np.broadcast_to(values.astype(np.float32)[:, None], (len(values), 128))

    def lanes(values):
        return np.broadcast_to(values.astype(np.float32)[None, :], (8, len(values)))

    columns = np.stack([column(v) for v in (order[::ROWS], offset[::ROWS], order[:ROWS], offset[:ROWS])])
    return jnp.asarray(columns), jnp.asarray(np.stack([lanes(order), lanes(offset)]))


def angles_by_row(columns, lon_count, big, small):
    rows = big.shape[1]
    lon = lax.broadcasted_iota(jnp.int32, (rows, lon_count), 1).astype(F32)
    phase = columns[0][:, 0:1] * lon + columns[1][:, 0:1]
    big[0] = cosine_of(phase, lon_count)
    big[1] = cosine_of(phase + 0.75 * lon_count, lon_count)
    lon = lax.broadcasted_iota(jnp.int32, (ROWS, lon_count), 1).astype(F32)
    phase = columns[2][:, 0:1] * lon + columns[3][:, 0:1]
    factor = 1.0 / math.sqrt(lon_count)
    small[0] = cosine_of(phase, lon_count) * factor
    small[1] = cosine_of(phase + 0.75 * lon_count, lon_count) * factor


def angles_by_lane(lanes, lon_count, big, small):
    rows, total = big.shape[1:]
    order, offset = lanes[0, 0:1, :], lanes[1, 0:1, :]
    lon = lax.broadcasted_iota(jnp.int32, (rows, total), 0).astype(F32) * float(ROWS)
    phase = lon * order
    big[0] = cosine_of(phase, lon_count)
    big[1] = cosine_of(phase + 0.75 * lon_count, lon_count)
    lon = lax.broadcasted_iota(jnp.int32, (ROWS, total), 0).astype(F32)
    phase = lon * order + offset
    factor = 1.0 / math.sqrt(lon_count)
    small[0] = cosine_of(phase, lon_count) * factor
    small[1] = cosine_of(phase + 0.75 * lon_count, lon_count) * factor


def fill(dst, big, small, first, last):
    def step(h, carry):
        value = big[0, pl.ds(h, 1), :] * small[0] - big[1, pl.ds(h, 1), :] * small[1]
        dst[pl.ds(pl.multiple_of(h * ROWS, ROWS), ROWS), :] = value.astype(BF16)
        return carry

    lax.fori_loop(first, last, step, 0)


def alpha_column(section, rows, span):
    row = lax.broadcasted_iota(jnp.int32, (rows, 128), 0)
    zero = jnp.logical_or(row == 0, row == span // 2)
    alpha = jnp.where(zero, 1.0, 2.0) if section == 0 else jnp.full((rows, 128), 2.0, F32)
    return alpha[:, 0:1]


def section_product(table, wide, out, section, lanes, scaled):
    devices, _, span, width = out.shape
    count = devices * span
    chunk = 256
    each = chunk // span
    for q in range(count // chunk):
        first = section * count + q * chunk
        value = jnp.dot(
            table[first : first + chunk, :], wide[:, lanes], preferred_element_type=F32
        )
        if scaled:
            value = value * (alpha_column(0, chunk, span) if first == 0 else 2.0)
        out[q * each : (q + 1) * each, section] = value.astype(BF16).reshape(each, span, width)


def legendre_tables(
    slot_ref, start_ref, lat_ref, synth, anal, tsynth, tanal, hold
):
    groups, width = slot_ref.shape
    orders = slot_ref[...] + lax.axis_index("space").astype(F32)
    order_sq = orders * orders
    cosine = lat_ref[0:1, :]
    wrow = lat_ref[1:2, :]
    wcol = jnp.broadcast_to(wrow, (128, width)).T[:, 0:1]
    block = 32

    def degree_block(index, carry):
        p_now, p_prev, e_prev, log_scale = carry
        scale = jnp.exp(log_scale)
        base = index * block
        for inner in range(block):
            degree_int = base + inner
            degree = degree_int.astype(F32)
            active = degree > orders
            square = degree * degree
            ratio = jnp.maximum(square - order_sq, 1.0) / jnp.maximum(4.0 * square - 1.0, 1.0)
            coef = lax.rsqrt(ratio)
            p_next = jnp.where(active, coef * (cosine * p_now - e_prev * p_prev), p_now)
            p_prev = jnp.where(active, p_now, p_prev)
            e_prev = jnp.where(active, ratio * coef, 0.0)
            p_now = p_next
            value = jnp.where(degree >= orders, p_now * scale, 0.0)
            rows = pl.ds(pl.multiple_of(degree_int * groups, groups), groups)
            for part in range(width // 128):
                hold[part, rows, :] = value[:, part * 128 : (part + 1) * 128]
        magnitude = jnp.maximum(jnp.abs(p_now), jnp.abs(p_prev))
        return (p_now / magnitude, p_prev / magnitude, e_prev, log_scale + jnp.log(magnitude))

    ones = jnp.ones((groups, width), F32)
    zeros = jnp.zeros((groups, width), F32)
    lax.fori_loop(0, MODES // block, degree_block, (ones, zeros, zeros, start_ref[...]))

    def spread(g, carry):
        pieces = [
            hold[part, pl.ds(g, MODES, stride=groups), :]
            for part in range(width // 128)
        ]
        value = pieces[0] if len(pieces) == 1 else jnp.concatenate(pieces, 1)
        synth[g] = value.astype(BF16)
        anal[g] = (value * wrow).astype(BF16)
        turned = value.T
        tsynth[g] = turned.astype(BF16)
        tanal[g] = (turned * wcol).astype(BF16)
        return carry

    lax.fori_loop(0, synth.shape[0], spread, 0)


def unpack(sources, parts, scratch, q):
    for src, (low, high) in zip(sources, parts):
        devices, _, span, _ = src.shape
        for a in range(low, high):
            part = src[:, q, :, (a - low) * 128 : (a - low + 1) * 128].astype(F32)
            scratch[a, q * devices * span : (q + 1) * devices * span] = part.reshape(
                devices * span, 128
            )


def pack(scratch, targets, parts, q):
    for dst, (low, high) in zip(targets, parts):
        devices, _, span, _ = dst.shape
        for a in range(low, high):
            part = scratch[a, q * devices * span : (q + 1) * devices * span]
            dst[:, q, :, (a - low) * 128 : (a - low + 1) * 128] = part.reshape(
                devices, span, 128
            ).astype(BF16)


def strided_rows(s, r, devices, span):
    half = span // 2
    start = s // half * (devices * span) + r * half + s % half
    return pl.ds(start, devices, stride=span)


def gather_group(scratch, g, devices, span, per_group, height):
    lat_local = scratch.shape[0]
    rows = []
    for j in range(per_group):
        s = g * per_group + j
        halves = []
        for r in range(2):
            pick = strided_rows(s, r, devices, span)
            parts = [scratch[a, pick, :] for a in range(lat_local)]
            if height > devices * lat_local:
                parts.append(jnp.zeros((height - devices * lat_local, 128), F32))
            halves.append(jnp.concatenate(parts, 0))
        zero = jnp.zeros((height, 256), F32)
        cells = [zero] * per_group
        cells[j] = jnp.concatenate(halves, 1)
        rows.append(cells[0] if per_group == 1 else jnp.concatenate(cells, 1))
    return (rows[0] if per_group == 1 else jnp.concatenate(rows, 0)).astype(BF16)


def scatter_group(value, scratch, g, devices, span, per_group, height):
    lat_local = scratch.shape[0]
    for j in range(per_group):
        s = g * per_group + j
        for r in range(2):
            for a in range(lat_local):
                top = j * height + a * devices
                left = j * 256 + r * 128
                scratch[a, strided_rows(s, r, devices, span), :] = value[
                    top : top + devices, left : left + 128
                ]


def over_groups(groups, sections, section, body):
    pieces = 4
    each = groups // pieces
    share = pieces // sections
    for q in range(section * share, (section + 1) * share):
        first = q * (MODES // pieces)
        lax.fori_loop(q * each, (q + 1) * each, functools.partial(body, first), 0)


def widen(filter_ref, first, copies):
    gain = filter_ref[first:, :].astype(F32)
    return jnp.concatenate([gain] * copies, 1)


def forward_body(per_group, shapes, anal, tsynth, filt, weight, scratch, back):
    devices, _, span, _ = shapes
    height = anal.shape[2] // per_group

    def body(first, g, carry):
        operand = gather_group(scratch, g, devices, span, per_group, height)
        spectrum = jnp.dot(anal[g, first:, :], operand, preferred_element_type=F32).astype(BF16)
        scaled = (spectrum.astype(F32) * widen(filt, first, 2 * per_group)).astype(BF16)
        mixed = [
            jnp.dot(
                scaled[:, j * 256 : (j + 1) * 256], weight[...], preferred_element_type=F32
            ).astype(BF16)
            for j in range(per_group)
        ]
        mixed = mixed[0] if per_group == 1 else jnp.concatenate(mixed, 1)
        value = jnp.dot(tsynth[g, :, first:], mixed, preferred_element_type=F32)
        scatter_group(value, back, g, devices, span, per_group, height)
        return carry

    return body


def backward_body(
    per_group, shapes, anal, synth, tanal, filt, weight, scratch, gscratch, wgrad, fgrad
):
    devices, _, span, _ = shapes
    height = anal.shape[2] // per_group

    def body(first, g, carry):
        operand = gather_group(scratch, g, devices, span, per_group, height)
        goperand = gather_group(gscratch, g, devices, span, per_group, height)
        gain = widen(filt, first, 2)
        outs = []
        spectrum = jnp.dot(anal[g, first:, :], operand, preferred_element_type=F32).astype(BF16)
        gmixed = jnp.dot(synth[g, first:, :], goperand, preferred_element_type=F32).astype(BF16)
        for j in range(per_group):
            lanes = slice(j * 256, (j + 1) * 256)
            spec = spectrum[:, lanes].astype(F32)
            scaled = (spec * gain).astype(BF16)
            gmix = gmixed[:, lanes]
            wgrad[...] += lax.dot_general(
                scaled, gmix, (((0,), (0,)), ((), ())), preferred_element_type=F32
            )
            gscaled = lax.dot_general(
                gmix, weight[...], (((1,), (1,)), ((), ())), preferred_element_type=F32
            )
            term = gscaled * spec
            fgrad[first:, :] += term[:, :128] + term[:, 128:]
            outs.append((gscaled * gain).astype(BF16))
        gspectrum = outs[0] if per_group == 1 else jnp.concatenate(outs, 1)
        value = jnp.dot(tanal[g, :, first:], gspectrum, preferred_element_type=F32)
        scatter_group(value, scratch, g, devices, span, per_group, height)
        return carry

    return body


def fold_gradients(wgrad, fgrad, red):
    half = wgrad.shape[0] // 2
    pieces = [
        (wgrad[:half, :half] + wgrad[half:, half:]) * (1.0 / MODES),
        (wgrad[:half, half:] - wgrad[half:, :half]) * (1.0 / MODES),
        fgrad[...] * 0.125,
    ]
    spare = red.shape[0] * red.shape[1] - 2 * half - MODES
    if spare:
        pieces.append(jnp.zeros((spare, 128), F32))
    red[...] = jnp.concatenate(pieces, 0).reshape(red.shape)


def gelu_slope(field):
    return 0.5 * (1.0 + lax.erf(field * (1.0 / math.sqrt(2.0)))) + field * jnp.exp(
        -0.5 * field * field
    ) * (1.0 / math.sqrt(2.0 * math.pi))


LON_CHUNK = 288


def merged(src, first, last, scaled):
    devices, _, span, width = src.shape
    pieces = []
    for q in range(first, last):
        value = src[:, q].astype(F32).reshape(devices * span, width)
        if scaled:
            value = value * alpha_column(q, devices * span, span)
        pieces.append(value.astype(BF16))
    return pieces[0] if len(pieces) == 1 else jnp.concatenate(pieces, 0)


def add_sections(ttable, operand, first, field, lanes, last):
    count = operand.shape[0]
    lon_count = field.shape[0]

    def grid_rows(q, carry):
        rows = pl.ds(pl.multiple_of(q * LON_CHUNK, LON_CHUNK), LON_CHUNK)
        value = jnp.dot(
            ttable[rows, first : first + count], operand, preferred_element_type=F32
        )
        if first:
            value = value + field[rows, lanes]
        if last is None:
            field[rows, lanes] = value
        else:
            last(q, rows, value)
        return carry

    lax.fori_loop(0, lon_count // LON_CHUNK, grid_rows, 0)


def lat_parts(lat_local):
    tail = max(1, lat_local // 3)
    if lat_local <= tail:
        return [(0, lat_local)]
    return [(0, lat_local - tail), (lat_local - tail, lat_local)]


def lane_slice(part):
    return slice(part[0] * 128, part[1] * 128)


def block_kernel(
    per_group,
    columns_hbm, lanes_hbm, grid_hbm, upstream_hbm, slots_hbm, start_hbm, lats_hbm, filt_hbm, mix_hbm,
    grad_hbm, sums_hbm,
    columns, lanes, grid, upstream, slots, start, lats, filt, mix_weight, grad,
    weight, total, table, ttable, big, small, tbig, tsmall,
    synth, anal, tsynth, tanal, hold,
    scratch, back, field, slope, wgrad, fgrad, red, stage, inbox,
    rsend, rrecv, lsem, osem,
    *buffers,
):
    lat_local = grid_hbm.shape[0]
    parts = lat_parts(lat_local)
    whole = [(0, lat_local)]
    split = len(parts)
    exchanges = [Exchange(*buffers[k : k + 4]) for k in range(0, len(buffers), 4)]
    first, fourth = exchanges[:2]
    second, third = exchanges[2 : 2 + split], exchanges[2 + split :]
    shapes = first.source.shape
    devices, sections, span, _ = shapes
    halves = [(0, sections // 2), (sections // 2, sections)] if sections > 1 else [(0, 1)]
    lat_local, lon_count, channels = grid_hbm.shape
    groups = synth.shape[0]
    me = lax.axis_index("space")
    greet(devices)

    loads = {}

    def load(name, src, dst):
        copy = pltpu.make_async_copy(src, dst, lsem.at[len(loads)])
        copy.start()
        loads[name] = copy

    load("columns", columns_hbm, columns)
    for a in range(lat_local):
        load(("grid", a), grid_hbm.at[a], grid.at[:, a * 128 : (a + 1) * 128])
    load("slots", slots_hbm, slots)
    load("start", start_hbm.at[me], start)
    load("lats", lats_hbm, lats)
    load("filt", filt_hbm, filt)
    load("mix", mix_hbm, mix_weight)
    load("lanes", lanes_hbm, lanes)
    for a in range(lat_local):
        load(("up", a), upstream_hbm.at[a], upstream.at[:, a * 128 : (a + 1) * 128])

    everything = slice(0, lat_local * 128)
    loads["columns"].wait()
    angles_by_row(columns, lon_count, big, small)
    share = big.shape[1] // sections
    for q in range(sections):
        fill(table, big, small, q * share, (q + 1) * share)
        if q == 0:
            for a in range(lat_local):
                loads["grid", a].wait()
        section_product(table, grid, first.source, q, everything, False)
        if q == 0:
            await_greetings(devices)
        first.send(q, q + 1)
    for name in ("slots", "start", "lats", "filt", "mix", "lanes"):
        loads[name].wait()
    weight[:channels, :channels] = mix_weight[0]
    weight[:channels, channels:] = mix_weight[1]
    weight[channels:, :channels] = -mix_weight[1]
    weight[channels:, channels:] = mix_weight[0]
    legendre_tables(slots, start, lats, synth, anal, tsynth, tanal, hold)

    forward = forward_body(per_group, shapes, anal, tsynth, filt, weight, scratch, back)
    for low, high in halves:
        for q in range(low, high):
            first.arrive(q, q + 1)
            unpack([first.target], whole, scratch, q)
            over_groups(groups, sections, q, forward)
            pack(back, [exchange.source for exchange in second], parts, q)
        second[0].send(low, high)
    for exchange in second[1:]:
        exchange.send(0, sections)
    angles_by_lane(lanes, lon_count, tbig, tsmall)
    fill(ttable, tbig, tsmall, 0, tbig.shape[1])
    for a in range(lat_local):
        loads["up", a].wait()

    def gate(where, q, rows, value):
        up = upstream[rows, where].astype(F32)
        slope[rows, where] = (up * gelu_slope(value)).astype(BF16)

    for p, part in enumerate(parts):
        where = lane_slice(part)
        close = functools.partial(gate, where)
        for low, high in halves if p == 0 else [(0, sections)]:
            second[p].arrive(low, high)
            operand = merged(second[p].target, low, high, True)
            last = close if high == sections else None
            add_sections(ttable, operand, low * devices * span, field, where, last)
        for low, high in halves:
            for q in range(low, high):
                section_product(table, slope, third[p].source, q, where, True)
            if p == 0 and low == 0 or split == 1:
                third[p].send(low, high)
            if p == split - 1 and p > 0:
                for exchange in third if low else third[1:]:
                    exchange.send(low, high)

    wgrad[...] = jnp.zeros_like(wgrad)
    fgrad[...] = jnp.zeros_like(fgrad)
    backward = backward_body(
        per_group, shapes, anal, synth, tanal, filt, weight, scratch, back, wgrad, fgrad
    )
    for low, high in halves:
        for exchange in third:
            exchange.arrive(low, high)
        for q in range(low, high):
            unpack([exchange.target for exchange in third], parts, back, q)
            over_groups(groups, sections, q, backward)
            pack(scratch, [fourth.source], whole, q)
            if low == 0 and sections > 1:
                fourth.send(q, q + 1)
    fold_gradients(wgrad, fgrad, red)
    reduction = Reduction(red, stage, inbox, total, rsend, rrecv)

    def out_copy(q, a, rows):
        return pltpu.make_async_copy(
            grad.at[rows, a * 128 : (a + 1) * 128], grad_hbm.at[a, rows, :], osem.at[q, a]
        )

    def finish(q, rows, value):
        grad[rows, :] = (value + upstream[rows, :].astype(F32)).astype(BF16)
        for a in range(lat_local):
            out_copy(q, a, rows).start()

    def tail(low, high):
        fourth.arrive(low, high)
        operand = merged(fourth.target, low, high, False)
        last = finish if high == sections else None
        add_sections(ttable, operand, low * devices * span, field, everything, last)

    steps = reduction.steps()
    middle = len(steps) // 2
    held = list(range(*halves[-1]))
    sends = {q: min(middle - 1 + k, middle) for k, q in enumerate(held)}
    places = {q: min(middle - 1 + q, len(steps) - 1) for q in range(sections - 1)}
    for index, (begin, end, level) in enumerate(steps):
        copies = begin(level)
        for copy in copies:
            copy.start()
        for q in held:
            if sends[q] == index:
                fourth.send(q, q + 1)
        for q, place in places.items():
            if place == index:
                tail(q, q + 1)
        end(level, copies)
    red[...] = total[...].astype(F32)
    sums_copy = pltpu.make_async_copy(red, sums_hbm, lsem.at[len(loads)])
    sums_copy.start()
    for exchange in (first, *second, *third):
        exchange.drain()
    tail(sections - 1, sections)
    fourth.drain()
    for q in range(lon_count // LON_CHUNK):
        rows = pl.ds(q * LON_CHUNK, LON_CHUNK)
        for a in range(lat_local):
            out_copy(q, a, rows).wait()
    sums_copy.wait()


def publish_kernel(grad_in, sums_in, grad, weight, filt, grad_v, sums_v, isem, osem):
    lat_local = grad_in.shape[0]
    pulls = [
        pltpu.make_async_copy(grad_in.at[a], grad_v.at[a], isem.at[a]) for a in range(lat_local)
    ]
    pulls.append(pltpu.make_async_copy(sums_in, sums_v, isem.at[lat_local]))
    for copy in pulls:
        copy.start()
    pushes = []
    for a in range(lat_local):
        pulls[a].wait()
        pushes.append(pltpu.make_async_copy(grad_v.at[a], grad.at[a], osem.at[a]))
        pushes[-1].start()
    pulls[-1].wait()
    rows = weight.shape[1]
    for r in range(weight.shape[0]):
        pushes.append(
            pltpu.make_async_copy(
                sums_v.at[pl.ds(r * rows, rows)], weight.at[r], osem.at[lat_local + r]
            )
        )
    pushes.append(
        pltpu.make_async_copy(
            sums_v.at[pl.ds(2 * rows, filt.shape[0])], filt, osem.at[lat_local + weight.shape[0]]
        )
    )
    for copy in pushes[lat_local:]:
        copy.start()
    for copy in pushes:
        copy.wait()


def order_logs(devices, group_orders, sines):
    scale = []
    for m in range(MODES):
        value = 0.5 * (math.log(2.0 * m + 1.0) - math.log(2.0))
        value += 0.5 * (math.lgamma(2.0 * m + 1.0) - 2.0 * math.lgamma(m + 1.0) - m * math.log(4.0))
        scale.append(value)
    orders = group_orders[None] + np.arange(devices)[:, None, None]
    return (np.array(scale)[orders] + orders * np.log(sines)[None, None, :]).astype(np.float32)


def body(grid_in, upstream, mix_weight, degree_filter):
    devices = lax.axis_size("space")
    me = lax.axis_index("space")
    lat_local, lon_count, channels = grid_in.shape
    lat_count = lat_local * devices
    slots = MODES // devices
    sections = sections_of(devices)
    span = 2 * slots // sections
    height = 64 if lat_count <= 64 else -(-lat_count // 128) * 128
    per_group = 128 // height if height < 128 else 1
    width = height * per_group
    groups = slots // per_group
    dims = (devices, sections, span)

    lane = np.arange(width)
    within = lane % height
    valid = within < lat_count
    latitude = np.where(valid, within % devices * lat_local + within // devices, 0)
    padded = -(-groups // 8) * 8
    group = np.minimum(np.arange(padded), groups - 1)[:, None]
    group_orders = (group * per_group + lane[None, :] // height) * devices
    slot_orders = jnp.asarray(group_orders.astype(np.float32))
    angles = math.pi * (latitude + 0.5) / lat_count
    start = jnp.asarray(order_logs(devices, group_orders, np.sin(angles)))
    weights = math.pi / lat_count * np.sin(angles) * valid
    lats = np.stack([np.cos(angles)] + [weights] * 7).astype(np.float32)
    columns, lanes = angle_indices(devices, lon_count)
    operands = (
        columns, lanes, grid_in, upstream, slot_orders, start, jnp.asarray(lats), degree_filter, mix_weight,
    )

    share = -(-(2 * channels + MODES) // (16 * devices)) * 16
    blocks = (devices, share, channels)
    vmem = pltpu.VMEM
    slab = vmem((lat_local, 2 * MODES, 128), F32)
    total_rows = 2 * MODES
    wide = lat_local * channels
    semaphores = pltpu.SemaphoreType.DMA((sections, devices))
    buffers = []
    for low, high in [(0, lat_local)] * 2 + lat_parts(lat_local) * 2:
        block = vmem((*dims, (high - low) * channels), BF16)
        buffers += [block, block, semaphores, semaphores]
    levels = radices_of(devices)
    hops = pltpu.SemaphoreType.DMA((2, len(levels), max(levels)))
    anywhere = pl.BlockSpec(memory_space=pl.ANY)
    grad, sums = pl.pallas_call(
        functools.partial(block_kernel, per_group),
        out_shape=(
            jax.ShapeDtypeStruct(grid_in.shape, BF16),
            jax.ShapeDtypeStruct(blocks, F32),
        ),
        in_specs=[anywhere] * len(operands),
        out_specs=(anywhere, anywhere),
        scratch_shapes=[
            vmem(columns.shape, F32),
            vmem(lanes.shape, F32),
            vmem((lon_count, wide), BF16),
            vmem((lon_count, wide), BF16),
            vmem(slot_orders.shape, F32),
            vmem(start.shape[1:], F32),
            vmem(lats.shape, F32),
            vmem(degree_filter.shape, BF16),
            vmem(mix_weight.shape, BF16),
            vmem((lon_count, wide), BF16),
            vmem((2 * channels, 2 * channels), BF16),
            vmem(blocks, BF16),
            vmem((total_rows, lon_count), BF16),
            vmem((lon_count, total_rows), BF16),
            vmem((2, total_rows // ROWS, lon_count), F32),
            vmem((2, ROWS, lon_count), F32),
            vmem((2, lon_count // ROWS, total_rows), F32),
            vmem((2, ROWS, total_rows), F32),
            vmem((groups, MODES, width), BF16),
            vmem((groups, MODES, width), BF16),
            vmem((groups, width, MODES), BF16),
            vmem((groups, width, MODES), BF16),
            vmem((width // 128, MODES * padded, 128), F32),
            slab,
            slab,
            vmem((lon_count, wide), F32),
            vmem((lon_count, wide), BF16),
            vmem((2 * channels, 2 * channels), F32),
            vmem((MODES, channels), F32),
            vmem(blocks, F32),
            vmem(blocks, BF16),
            vmem(blocks, BF16),
            hops,
            hops,
            pltpu.SemaphoreType.DMA((16 + 2 * lat_local,)),
            pltpu.SemaphoreType.DMA((lon_count // LON_CHUNK, lat_local)),
            *buffers,
        ],
        compiler_params=params(collective_id=0, has_side_effects=True),
        name="block",
    )(*operands)
    flat = sums.reshape(devices * share, channels)
    return pl.pallas_call(
        publish_kernel,
        out_shape=(
            jax.ShapeDtypeStruct(grid_in.shape, BF16),
            jax.ShapeDtypeStruct(mix_weight.shape, F32),
            jax.ShapeDtypeStruct(degree_filter.shape, F32),
        ),
        in_specs=[anywhere, anywhere],
        out_specs=(anywhere,) * 3,
        scratch_shapes=[
            vmem(grid_in.shape, BF16),
            vmem(flat.shape, F32),
            pltpu.SemaphoreType.DMA((lat_local + 1,)),
            pltpu.SemaphoreType.DMA((lat_local + 3,)),
        ],
        name="publish",
    )(grad, flat)


def solution(mesh):
    return jax.shard_map(
        body,
        mesh=mesh,
        in_specs=(P(("groups", "space"), None, None), P(("groups", "space"), None, None), P(), P()),
        out_specs=(P(("groups", "space"), None, None), P("groups", None, None), P("groups", None)),
        check_vma=False,
    )
```
